32 devices in a mesh: parts: 2 (over x), slab: 8 (over z, y), freq: 2 (over core).
Axes of the slice: x: 2, y: 2, z: 4, core: 2. Of those that a mesh axis runs over, the one named last changes fastest.
Arguments:
- reflectivity: float32 [65536], P(('parts', 'slab')), parts along dimension 0, may hold values from -6 to 6
- source_green: bfloat16 [4, 65536, 2, 256], P('freq', ('parts', 'slab')), parts along dimension 1, may hold values from -6 to 6
- receiver_green: bfloat16 [4, 65536, 2, 256], P('freq', ('parts', 'slab')), parts along dimension 1, may hold values from -0.03125 to 0.03125
- observed: float32 [4, 32, 2, 128, 128], P('freq', ('parts', 'slab')), parts along dimension 1, may hold values from -6 to 6
- source_table: int32 [16, 2], P(('parts', 'slab')), parts along dimension 0, may hold values from 0 to 3, as said below
- receiver_table: int32 [16, 2], P(('parts', 'slab')), parts along dimension 0, may hold values from 0 to 3, as said below
Outputs:
- gradient: float32 [65536], P(('parts', 'slab', 'freq')), parts along dimension 0
- residual: float32 [4, 32, 2, 128, 128], P('freq', ('parts', 'slab')), parts along dimension 1
The draws below stay inside these ranges and needn't reach their ends.
There are 2 independent parts, one for each index of `parts`. The reference program is written for one: setup_inputs(seed, part) draws one part's arguments, and reference() takes and returns one part's arrays. A program takes and returns all parts, laid end to end along the dimension named above; each array names one. Nothing has to cross between parts.
Inputs may be any that keep to these rules, and one draw needn't show every extreme that they name: `source_table`: each row lists 2 different source blocks. `receiver_table`: each row lists 2 different receiver blocks.
All inputs are finite; a program needn't handle non-finite values.
Results may differ from the reference program's by a relative error of at most 0.0016.
Values may be sent and summed in bfloat16 or wider, within the bound.
A program may use at most 128 MiB of HBM per device.

```python
import jax
import jax.numpy as jnp
from jax import lax

BLK = 128
FREQS = 4
SB = 4
RB = 4
KS = 2
KR = 2
M_DEV = 4096
SLABS = 8
M = 32768
PANELS = 16


def station_rows(key, row_count, block_count, take_count):
    subkeys = jax.random.split(key, row_count)
    shuffled = jax.vmap(lambda one_key: jax.random.permutation(one_key, block_count))(subkeys)[:, :take_count]
    anchored = (block_count - 1 + jnp.arange(take_count)) % block_count
    leading = jnp.arange(row_count)[:, None] == 0
    return jnp.where(leading, anchored[None, :], shuffled).astype(jnp.int32)


def draw_source_table(key, part):
    return station_rows(jax.random.fold_in(key, 11), SLABS, SB, KS)


def draw_receiver_table(key, part):
    return station_rows(jax.random.fold_in(key, 23), SLABS, RB, KR)


def steps_of(stream_key, shape, cuts, smallest, largest):
    gain, own = 1.0, jax.random.fold_in(stream_key, 6)
    for axis_at, shards_of in cuts:
        draws = jnp.exp(jax.random.uniform(jax.random.fold_in(own, axis_at), (shards_of,), jnp.float32, smallest / len(cuts), largest / len(cuts)))
        gain = gain * jnp.repeat(draws, shape[axis_at] // shards_of).reshape([-1 if axis == axis_at else 1 for axis in range(len(shape))])
    return gain


def scatter_about(rng, shape, deviation, reach, cuts=(), kind=jnp.bfloat16):
    result = deviation * jax.random.normal(rng, shape, jnp.float32)
    if cuts:
        result = result * steps_of(rng, shape, cuts, -0.22, 0.18)
    return jnp.clip(result, -reach, reach).astype(kind)


def setup_inputs(seed: int = 0, part: int = 0) -> dict:
    key_of = jax.random.split(jax.random.key(seed), 7)
    own_keys = jax.random.split(jax.random.fold_in(key_of[6], part), 7)
    reflectivity = scatter_about(own_keys[0], (M,), 1.0, 6.0, ((0, 8),), jnp.float32)
    source_green = scatter_about(own_keys[1], (FREQS, M, 2, KS * BLK), 1.0, 6.0, ((0, 2), (1, 8)))
    receiver_green = scatter_about(own_keys[2], (FREQS, M, 2, KR * BLK), (8 * M_DEV) ** -0.5, 0.03125, ((0, 2), (1, 8)))
    observed = scatter_about(own_keys[3], (FREQS, PANELS, 2, BLK, BLK), 1.0, 6.0, ((0, 2), (1, 8)), jnp.float32)
    source_table = draw_source_table(jax.random.fold_in(jax.random.fold_in(key_of[6], part), 71), part)
    receiver_table = draw_receiver_table(jax.random.fold_in(jax.random.fold_in(key_of[6], part), 71), part)
    return {"reflectivity": reflectivity, "source_green": source_green, "receiver_green": receiver_green, "observed": observed, "source_table": source_table, "receiver_table": receiver_table}


def panel_ids_of(src_row, rec_row):
    return (src_row[:, None] * RB + rec_row[None, :]).reshape(-1).astype(jnp.int32)


def forward_panels(scaled_slab, rec_slab):
    products = jnp.einsum('fmas,fmbr->fasbr', scaled_slab.astype(jnp.float32), rec_slab.astype(jnp.float32))
    real_part = products[:, 0, :, 0, :] - products[:, 1, :, 1, :]
    imag_part = products[:, 0, :, 1, :] + products[:, 1, :, 0, :]
    stacked = jnp.stack([real_part, imag_part], axis=1)
    stacked = stacked.reshape(FREQS, 2, KS, BLK, KR, BLK).transpose(0, 2, 4, 1, 3, 5)
    return stacked.reshape(FREQS, KS * KR, 2, BLK, BLK)


def reference(reflectivity, source_green, receiver_green, observed, source_table, receiver_table):
    scaled = (source_green * reflectivity[None, :, None, None]).astype(jnp.bfloat16)
    slab_ids = jnp.arange(SLABS, dtype=jnp.int32)

    def add_slab(predicted, slab_id):
        first_point = (slab_id * M_DEV).astype(jnp.int32)
        scaled_slab = lax.dynamic_slice_in_dim(scaled, first_point, M_DEV, 1)
        rec_slab = lax.dynamic_slice_in_dim(receiver_green, first_point, M_DEV, 1)
        partial_value = forward_panels(scaled_slab, rec_slab)
        panel_ids = panel_ids_of(source_table[slab_id], receiver_table[slab_id])
        return predicted.at[:, panel_ids].add(partial_value), None

    start_pred = jnp.zeros((FREQS, PANELS, 2, BLK, BLK), jnp.float32)
    predicted, unused = lax.scan(add_slab, start_pred, slab_ids)
    residual = predicted - observed
    rounded = residual.astype(jnp.bfloat16)

    def slab_gradient(slab_id):
        first_point = (slab_id * M_DEV).astype(jnp.int32)
        src_slab = lax.dynamic_slice_in_dim(source_green, first_point, M_DEV, 1).astype(jnp.float32)
        rec_slab = lax.dynamic_slice_in_dim(receiver_green, first_point, M_DEV, 1).astype(jnp.float32)
        panel_ids = panel_ids_of(source_table[slab_id], receiver_table[slab_id])
        local_res = rounded[:, panel_ids].astype(jnp.float32)
        local_res = local_res.reshape(FREQS, KS, KR, 2, BLK, BLK).transpose(0, 1, 4, 3, 2, 5)
        local_res = local_res.reshape(FREQS, KS * BLK, 2, KR * BLK)
        products = jnp.einsum('fmas,fsbr->fmabr', src_slab, local_res)
        adj_real = products[:, :, 0, 0] + products[:, :, 1, 1]
        adj_imag = products[:, :, 0, 1] - products[:, :, 1, 0]
        slab_grad = rec_slab[:, :, 0] * adj_real + rec_slab[:, :, 1] * adj_imag
        return jnp.sum(slab_grad, axis=(0, 2))

    gradient = lax.map(slab_gradient, slab_ids).reshape(-1)
    return gradient, residual
```

```python
import functools

import jax
import jax.numpy as jnp
from jax import lax
from jax.experimental import pallas as pl
from jax.experimental.pallas import tpu as pltpu
from jax.sharding import PartitionSpec as P

RB = 4
TILE = 1024
MESH = pl.DeviceIdType.MESH
F32 = jnp.float32
BF16 = jnp.bfloat16


def forward_kernel(refl_ref, g_ref, r_ref, gd_ref, rd_ref, part_ref, g32, r32, scaled, acc):
    step = pl.program_id(1)
    lanes = g_ref.shape[2]
    points = gd_ref.shape[1]
    half = gd_ref.shape[2] // 2
    blocks = half // lanes
    rows_each = 2 * blocks
    g32[...] = g_ref[0].astype(F32)
    r32[...] = r_ref[0].astype(F32)
    weight = jnp.concatenate(
        [
            jnp.broadcast_to(refl_ref[b : b + 1, :], (lanes, lanes)).T
            for b in range(points // lanes)
        ],
        axis=0,
    )
    for block in range(blocks):
        for comp in range(2):
            rows = pl.ds(block * 2 + comp, points, stride=rows_each)
            cols = slice(comp * half + block * lanes, comp * half + (block + 1) * lanes)
            green = g32[rows, :]
            gd_ref[0, :, cols] = green.astype(BF16)
            scaled[:, cols] = (green * weight).astype(BF16)
            rd_ref[0, :, cols] = r32[rows, :].astype(BF16)
    prod = lax.dot_general(
        scaled[...], rd_ref[0], (((0,), (0,)), ((), ())), preferred_element_type=F32
    )

    @pl.when(step == 0)
    def _():
        acc[...] = prod

    @pl.when(step > 0)
    def _():
        acc[...] += prod

    @pl.when(step == pl.num_programs(1) - 1)
    def _():
        for i in range(blocks):
            for j in range(blocks):
                s_re = slice(i * lanes, (i + 1) * lanes)
                s_im = slice(half + i * lanes, half + (i + 1) * lanes)
                r_re = slice(j * lanes, (j + 1) * lanes)
                r_im = slice(half + j * lanes, half + (j + 1) * lanes)
                part_ref[0, i * blocks + j, 0] = acc[s_re, r_re] - acc[s_im, r_im]
                part_ref[0, i * blocks + j, 1] = acc[s_re, r_im] + acc[s_im, r_re]
        part_ref[0, blocks * blocks] = jnp.zeros(part_ref.shape[2:], F32)


def ring_kernel(n, snake, table_ref, part_ref, obs_ref, res_ref, adj_ref, first, held, gath,
                rs_send, rs_recv, ag_send, ag_recv):
    per = obs_ref.shape[1]
    lanes = obs_ref.shape[3]
    pairs = part_ref.shape[1] - 1
    total = n * per
    me = lax.axis_index("slab")

    def index_of(pos):
        if not snake:
            return pos
        return 2 * pos + (pos // (n // 2)) * (2 * n - 1 - 4 * pos)

    if snake:
        place = me // 2 + (me % 2) * (n - 1 - 2 * (me // 2))
    else:
        place = me
    ways = (1, -1)
    targets = tuple(index_of((place + way + n) % n) for way in ways)

    barrier = pltpu.get_barrier_semaphore()
    for target in targets:
        pl.semaphore_signal(barrier, inc=1, device_id={"slab": target}, device_id_type=MESH)
    pl.semaphore_wait(barrier, 2)

    streams = [(f, c) for c in range(2) for f in range(2)]

    def own(f, c, hop):
        owner = index_of((place - ways[f] * hop + 2 * n) % n)
        return [part_ref[f, table_ref[owner * per + k], c] for k in range(per)]

    def rs_copy(f, c, src, step):
        return pltpu.make_async_remote_copy(
            src_ref=src,
            dst_ref=held.at[f, c, step],
            send_sem=rs_send.at[f, c, step],
            recv_sem=rs_recv.at[f, c, step],
            device_id={"slab": targets[f]},
            device_id_type=MESH,
        )

    def ag_copy(f, c, step):
        owner = index_of((place - ways[f] * step + 2 * n) % n)
        view = gath.at[f, c, pl.ds(owner * per, per)]
        return pltpu.make_async_remote_copy(
            src_ref=view,
            dst_ref=view,
            send_sem=ag_send.at[f, c, step],
            recv_sem=ag_recv.at[f, c, step],
            device_id={"slab": targets[f]},
            device_id_type=MESH,
        )

    def ag_wait(f, c, step):
        owner = index_of((place - ways[f] * (step + 1) + 2 * n) % n)
        view = gath.at[f, c, pl.ds(owner * per, per)]
        pltpu.make_async_remote_copy(
            src_ref=view,
            dst_ref=view,
            send_sem=ag_send.at[f, c, step],
            recv_sem=ag_recv.at[f, c, step],
            device_id={"slab": targets[f]},
            device_id_type=MESH,
        ).wait_recv()

    for f, c in streams:
        mine = own(f, c, 1)
        for k in range(per):
            first[f, c, k] = mine[k]
        rs_copy(f, c, first.at[f, c], 0).start()

    def rs_step(step, carry):
        for f, c in streams:
            rs_copy(f, c, held.at[f, c, step], step).wait_recv()
            mine = own(f, c, step + 2)
            for k in range(per):
                held[f, c, step, k] = held[f, c, step, k] + mine[k]
            rs_copy(f, c, held.at[f, c, step], step + 1).start()
        return carry

    lax.fori_loop(0, n - 2, rs_step, 0)
    for f, c in streams:
        rs_copy(f, c, held.at[f, c, n - 2], n - 2).wait_recv()
        mine = own(f, c, n)
        for k in range(per):
            value = held[f, c, n - 2, k] + mine[k] - obs_ref[f, k, c]
            res_ref[f, k, c] = value
            gath[f, c, me * per + k] = value.astype(BF16)
        ag_copy(f, c, 0).start()

    def ag_step(step, carry):
        for f, c in streams:
            ag_wait(f, c, step)
            ag_copy(f, c, step + 1).start()
        return carry

    lax.fori_loop(0, n - 2, ag_step, 0)
    for f, c in streams:
        ag_wait(f, c, n - 2)

    def drain(step, carry):
        for f, c in streams:
            rs_copy(f, c, first.at[f, c], step).wait_send()
            ag_copy(f, c, step).wait_send()
        return carry

    lax.fori_loop(0, n - 1, drain, 0)

    side = 2
    half = side * lanes
    for f in range(2):
        for k in range(pairs):
            i, j = k // side, k % side
            panel = table_ref[total + k]
            real = gath[f, 0, panel]
            imag = gath[f, 1, panel]
            s_re = slice(i * lanes, (i + 1) * lanes)
            s_im = slice(half + i * lanes, half + (i + 1) * lanes)
            r_re = slice(j * lanes, (j + 1) * lanes)
            r_im = slice(half + j * lanes, half + (j + 1) * lanes)
            adj_ref[f, s_re, r_re] = real
            adj_ref[f, s_im, r_re] = imag
            adj_ref[f, s_re, r_im] = imag
            adj_ref[f, s_im, r_im] = -real


def adjoint_kernel(gd_ref, rd_ref, adj_ref, out_ref, total):
    step = pl.program_id(1)
    lanes = out_ref.shape[1]
    width = gd_ref.shape[2]
    points = gd_ref.shape[1]
    field = jnp.dot(gd_ref[0], adj_ref[step], preferred_element_type=F32)
    terms = field * rd_ref[0].astype(F32)
    summed = terms[:, :lanes]
    for at in range(lanes, width, lanes):
        summed = summed + terms[:, at : at + lanes]

    @pl.when(step == 0)
    def _():
        total[...] = summed

    @pl.when(step > 0)
    def _():
        total[...] += summed

    @pl.when(step == pl.num_programs(1) - 1)
    def _():
        for b in range(points // lanes):
            block = total[b * lanes : (b + 1) * lanes, :]
            out_ref[b : b + 1, :] = jnp.sum(block.T, axis=0, keepdims=True)


def interleaved_rows(green, lanes):
    freqs, points, comps, width = green.shape
    view = green.reshape(freqs, points, comps, width // lanes, lanes)
    return view.transpose(0, 1, 3, 2, 4).reshape(freqs, points * comps * width // lanes, lanes)


def on_device(reflectivity, source_green, receiver_green, observed, source_table, receiver_table):
    freqs, points, comps, width = source_green.shape
    per = observed.shape[1]
    lanes = observed.shape[3]
    n = lax.axis_size("slab")
    side = width // lanes
    pairs = side * side
    wide = comps * width
    rows_each = wide // lanes
    tiles = points // TILE
    panel_ids = (source_table[0][:, None] * RB + receiver_table[0][None, :]).reshape(-1)
    slots = jnp.arange(n * per, dtype=jnp.int32)
    hit = slots[:, None] == panel_ids[None, :]
    where_held = jnp.min(
        jnp.where(hit, jnp.arange(pairs, dtype=jnp.int32)[None, :], pairs), axis=1
    )
    table = jnp.concatenate([where_held, panel_ids]).astype(jnp.int32)

    gd, rd, part = pl.pallas_call(
        forward_kernel,
        grid=(freqs, tiles),
        in_specs=[
            pl.BlockSpec((TILE // lanes, lanes), lambda f, t: (t, 0)),
            pl.BlockSpec((1, TILE * rows_each, lanes), lambda f, t: (f, t, 0)),
            pl.BlockSpec((1, TILE * rows_each, lanes), lambda f, t: (f, t, 0)),
        ],
        out_specs=[
            pl.BlockSpec((1, TILE, wide), lambda f, t: (f, t, 0)),
            pl.BlockSpec((1, TILE, wide), lambda f, t: (f, t, 0)),
            pl.BlockSpec((1, pairs + 1, 2, lanes, lanes), lambda f, t: (f, 0, 0, 0, 0)),
        ],
        out_shape=[
            jax.ShapeDtypeStruct((freqs, points, wide), BF16),
            jax.ShapeDtypeStruct((freqs, points, wide), BF16),
            jax.ShapeDtypeStruct((freqs, pairs + 1, 2, lanes, lanes), F32),
        ],
        scratch_shapes=[
            pltpu.VMEM((TILE * rows_each, lanes), F32),
            pltpu.VMEM((TILE * rows_each, lanes), F32),
            pltpu.VMEM((TILE, wide), BF16),
            pltpu.VMEM((wide, wide), F32),
        ],
        name="forward",
    )(
        reflectivity.reshape(points // lanes, lanes),
        interleaved_rows(source_green, lanes),
        interleaved_rows(receiver_green, lanes),
    )

    vmem = pl.BlockSpec(memory_space=pltpu.VMEM)
    residual, adj = pl.pallas_call(
        functools.partial(ring_kernel, n, n == 8),
        in_specs=[pl.BlockSpec(memory_space=pltpu.SMEM), vmem, vmem],
        out_specs=[vmem, vmem],
        out_shape=[
            jax.ShapeDtypeStruct(observed.shape, F32),
            jax.ShapeDtypeStruct((freqs, wide, wide), BF16),
        ],
        scratch_shapes=[
            pltpu.VMEM((freqs, 2, per, lanes, lanes), F32),
            pltpu.VMEM((freqs, 2, n - 1, per, lanes, lanes), F32),
            pltpu.VMEM((freqs, 2, n * per, lanes, lanes), BF16),
            pltpu.SemaphoreType.DMA((freqs, 2, n - 1)),
            pltpu.SemaphoreType.DMA((freqs, 2, n - 1)),
            pltpu.SemaphoreType.DMA((freqs, 2, n - 1)),
            pltpu.SemaphoreType.DMA((freqs, 2, n - 1)),
        ],
        compiler_params=pltpu.CompilerParams(collective_id=0, has_side_effects=True),
        name="ring",
    )(table, part, observed)

    gradient = pl.pallas_call(
        adjoint_kernel,
        grid=(tiles, freqs),
        in_specs=[
            pl.BlockSpec((1, TILE, wide), lambda t, f: (f, t, 0)),
            pl.BlockSpec((1, TILE, wide), lambda t, f: (f, t, 0)),
            pl.BlockSpec((freqs, wide, wide), lambda t, f: (0, 0, 0)),
        ],
        out_specs=pl.BlockSpec((TILE // lanes, lanes), lambda t, f: (t, 0)),
        out_shape=jax.ShapeDtypeStruct((points // lanes, lanes), F32),
        scratch_shapes=[pltpu.VMEM((TILE, lanes), F32)],
        name="adjoint",
    )(gd, rd, adj)
    gradient = gradient.reshape(points)
    return (lax.psum_scatter(gradient, "freq", scatter_dimension=0, tiled=True), residual)


def solution(mesh):
    return jax.shard_map(
        on_device,
        mesh=mesh,
        in_specs=(
            P(("parts", "slab")),
            P("freq", ("parts", "slab"), None, None),
            P("freq", ("parts", "slab"), None, None),
            P("freq", ("parts", "slab"), None, None, None),
            P(("parts", "slab"), None),
            P(("parts", "slab"), None),
        ),
        out_specs=(P(("parts", "slab", "freq")), P("freq", ("parts", "slab"), None, None, None)),
        check_vma=False,
    )
```

```python
import functools

import jax
import jax.numpy as jnp
from jax import lax
from jax.experimental import pallas as pl
from jax.experimental.pallas import tpu as pltpu
from jax.sharding import PartitionSpec as P

RB = 4
TILE = 1024
MESH = pl.DeviceIdType.MESH
F32 = jnp.float32
BF16 = jnp.bfloat16


def forward_kernel(refl_ref, g_ref, r_ref, gd_ref, rd_ref, part_ref, g32, r32, scaled, acc):
    step = pl.program_id(1)
    lanes = g_ref.shape[2]
    points = gd_ref.shape[1]
    half = gd_ref.shape[2] // 2
    blocks = half // lanes
    rows_each = 2 * blocks
    g32[...] = g_ref[0].astype(F32)
    r32[...] = r_ref[0].astype(F32)
    weight = jnp.concatenate(
        [
            jnp.broadcast_to(refl_ref[b : b + 1, :], (lanes, lanes)).T
            for b in range(points // lanes)
        ],
        axis=0,
    )
    for block in range(blocks):
        for comp in range(2):
            rows = pl.ds(block * 2 + comp, points, stride=rows_each)
            cols = slice(comp * half + block * lanes, comp * half + (block + 1) * lanes)
            green = g32[rows, :]
            gd_ref[0, :, cols] = green.astype(BF16)
            scaled[:, cols] = (green * weight).astype(BF16)
            rd_ref[0, :, cols] = r32[rows, :].astype(BF16)
    prod = lax.dot_general(
        scaled[...], rd_ref[0], (((0,), (0,)), ((), ())), preferred_element_type=F32
    )

    @pl.when(step == 0)
    def _():
        acc[...] = prod

    @pl.when(step > 0)
    def _():
        acc[...] += prod

    @pl.when(step == pl.num_programs(1) - 1)
    def _():
        for i in range(blocks):
            for j in range(blocks):
                s_re = slice(i * lanes, (i + 1) * lanes)
                s_im = slice(half + i * lanes, half + (i + 1) * lanes)
                r_re = slice(j * lanes, (j + 1) * lanes)
                r_im = slice(half + j * lanes, half + (j + 1) * lanes)
                part_ref[0, i * blocks + j, 0] = acc[s_re, r_re] - acc[s_im, r_im]
                part_ref[0, i * blocks + j, 1] = acc[s_re, r_im] + acc[s_im, r_re]
        part_ref[0, blocks * blocks] = jnp.zeros(part_ref.shape[2:], F32)


def ring_kernel(n, snake, table_ref, part_ref, obs_ref, res_ref, adj_ref, first, held, gath,
                rs_send, rs_recv, ag_send, ag_recv):
    per = obs_ref.shape[1]
    lanes = obs_ref.shape[3]
    pairs = part_ref.shape[1] - 1
    total = n * per
    me = lax.axis_index("slab")

    def index_of(pos):
        if not snake:
            return pos
        return 2 * pos + (pos // (n // 2)) * (2 * n - 1 - 4 * pos)

    if snake:
        place = me // 2 + (me % 2) * (n - 1 - 2 * (me // 2))
    else:
        place = me
    ways = (1, -1)
    targets = tuple(index_of((place + way + n) % n) for way in ways)
    low = (n - 1) // 2
    high = n - 1 - low

    barrier = pltpu.get_barrier_semaphore()
    for target in targets:
        pl.semaphore_signal(barrier, inc=1, device_id={"slab": target}, device_id_type=MESH)
    pl.semaphore_wait(barrier, 2)

    streams = [(f, c, w) for c in range(2) for f in range(2) for w in range(2)]
    longer = [(f, c, w) for f, c, w in streams if f == w]

    def hops(f, w):
        return high if f == w else low

    def own(f, c, w, away):
        owner = index_of((place + ways[w] * away + n) % n)
        return [part_ref[f, table_ref[owner * per + k], c] for k in range(per)]

    def rs_copy(f, c, w, src, step):
        return pltpu.make_async_remote_copy(
            src_ref=src,
            dst_ref=held.at[f, c, w, step],
            send_sem=rs_send.at[f, c, w, step],
            recv_sem=rs_recv.at[f, c, w, step],
            device_id={"slab": targets[w]},
            device_id_type=MESH,
        )

    def ag_copy(f, c, w, step, away):
        owner = index_of((place - ways[w] * away + n) % n)
        view = gath.at[f, c, pl.ds(owner * per, per)]
        return pltpu.make_async_remote_copy(
            src_ref=view,
            dst_ref=view,
            send_sem=ag_send.at[f, c, w, step],
            recv_sem=ag_recv.at[f, c, w, step],
            device_id={"slab": targets[w]},
            device_id_type=MESH,
        )

    def rs_pass(f, c, w, step):
        rs_copy(f, c, w, held.at[f, c, w, step], step).wait_recv()
        mine = own(f, c, w, hops(f, w) - step - 1)
        for k in range(per):
            held[f, c, w, step, k] = held[f, c, w, step, k] + mine[k]
        rs_copy(f, c, w, held.at[f, c, w, step], step + 1).start()

    def ag_pass(f, c, w, step):
        ag_copy(f, c, w, step, step + 1).wait_recv()
        ag_copy(f, c, w, step + 1, step + 1).start()

    def rs_step(step, carry):
        for f, c, w in streams:
            rs_pass(f, c, w, step)
        return carry

    def ag_step(step, carry):
        for f, c, w in streams:
            ag_pass(f, c, w, step)
        return carry

    for f, c, w in streams:
        mine = own(f, c, w, hops(f, w))
        for k in range(per):
            first[f, c, w, k] = mine[k]
        rs_copy(f, c, w, first.at[f, c, w], 0).start()

    lax.fori_loop(0, low - 1, rs_step, 0)
    if high > low:
        for f, c, w in longer:
            rs_pass(f, c, w, high - 2)
    for c in range(2):
        for f in range(2):
            for w in range(2):
                last = hops(f, w) - 1
                rs_copy(f, c, w, held.at[f, c, w, last], last).wait_recv()
            mine = own(f, c, 0, 0)
            for k in range(per):
                value = (
                    held[f, c, 0, hops(f, 0) - 1, k] + held[f, c, 1, hops(f, 1) - 1, k] + mine[k]
                ) - obs_ref[f, k, c]
                res_ref[f, k, c] = value
                gath[f, c, me * per + k] = value.astype(BF16)
            for w in range(2):
                ag_copy(f, c, w, 0, 0).start()

    lax.fori_loop(0, low - 1, ag_step, 0)
    if high > low:
        for f, c, w in longer:
            ag_pass(f, c, w, high - 2)
    for f, c, w in streams:
        last = hops(f, w) - 1
        ag_copy(f, c, w, last, last + 1).wait_recv()

    def drain(step, carry):
        for f, c, w in streams:
            rs_copy(f, c, w, first.at[f, c, w], step).wait_send()
            ag_copy(f, c, w, step, step).wait_send()
        return carry

    lax.fori_loop(0, low, drain, 0)
    if high > low:
        for f, c, w in longer:
            rs_copy(f, c, w, first.at[f, c, w], high - 1).wait_send()
            ag_copy(f, c, w, high - 1, high - 1).wait_send()

    side = 2
    half = side * lanes
    for f in range(2):
        for k in range(pairs):
            i, j = k // side, k % side
            panel = table_ref[total + k]
            real = gath[f, 0, panel]
            imag = gath[f, 1, panel]
            s_re = slice(i * lanes, (i + 1) * lanes)
            s_im = slice(half + i * lanes, half + (i + 1) * lanes)
            r_re = slice(j * lanes, (j + 1) * lanes)
            r_im = slice(half + j * lanes, half + (j + 1) * lanes)
            adj_ref[f, s_re, r_re] = real
            adj_ref[f, s_im, r_re] = imag
            adj_ref[f, s_re, r_im] = imag
            adj_ref[f, s_im, r_im] = -real


def adjoint_kernel(gd_ref, rd_ref, adj_ref, out_ref, total):
    step = pl.program_id(1)
    lanes = out_ref.shape[1]
    width = gd_ref.shape[2]
    points = gd_ref.shape[1]
    field = jnp.dot(gd_ref[0], adj_ref[step], preferred_element_type=F32)
    terms = field * rd_ref[0].astype(F32)
    summed = terms[:, :lanes]
    for at in range(lanes, width, lanes):
        summed = summed + terms[:, at : at + lanes]

    @pl.when(step == 0)
    def _():
        total[...] = summed

    @pl.when(step > 0)
    def _():
        total[...] += summed

    @pl.when(step == pl.num_programs(1) - 1)
    def _():
        for b in range(points // lanes):
            block = total[b * lanes : (b + 1) * lanes, :]
            out_ref[b : b + 1, :] = jnp.sum(block.T, axis=0, keepdims=True)


def interleaved_rows(green, lanes):
    freqs, points, comps, width = green.shape
    view = green.reshape(freqs, points, comps, width // lanes, lanes)
    return view.transpose(0, 1, 3, 2, 4).reshape(freqs, points * comps * width // lanes, lanes)


def on_device(reflectivity, source_green, receiver_green, observed, source_table, receiver_table):
    freqs, points, comps, width = source_green.shape
    per = observed.shape[1]
    lanes = observed.shape[3]
    n = lax.axis_size("slab")
    side = width // lanes
    pairs = side * side
    wide = comps * width
    rows_each = wide // lanes
    tiles = points // TILE
    panel_ids = (source_table[0][:, None] * RB + receiver_table[0][None, :]).reshape(-1)
    slots = jnp.arange(n * per, dtype=jnp.int32)
    hit = slots[:, None] == panel_ids[None, :]
    where_held = jnp.min(
        jnp.where(hit, jnp.arange(pairs, dtype=jnp.int32)[None, :], pairs), axis=1
    )
    table = jnp.concatenate([where_held, panel_ids]).astype(jnp.int32)

    gd, rd, part = pl.pallas_call(
        forward_kernel,
        grid=(freqs, tiles),
        in_specs=[
            pl.BlockSpec((TILE // lanes, lanes), lambda f, t: (t, 0)),
            pl.BlockSpec((1, TILE * rows_each, lanes), lambda f, t: (f, t, 0)),
            pl.BlockSpec((1, TILE * rows_each, lanes), lambda f, t: (f, t, 0)),
        ],
        out_specs=[
            pl.BlockSpec((1, TILE, wide), lambda f, t: (f, t, 0)),
            pl.BlockSpec((1, TILE, wide), lambda f, t: (f, t, 0)),
            pl.BlockSpec((1, pairs + 1, 2, lanes, lanes), lambda f, t: (f, 0, 0, 0, 0)),
        ],
        out_shape=[
            jax.ShapeDtypeStruct((freqs, points, wide), BF16),
            jax.ShapeDtypeStruct((freqs, points, wide), BF16),
            jax.ShapeDtypeStruct((freqs, pairs + 1, 2, lanes, lanes), F32),
        ],
        scratch_shapes=[
            pltpu.VMEM((TILE * rows_each, lanes), F32),
            pltpu.VMEM((TILE * rows_each, lanes), F32),
            pltpu.VMEM((TILE, wide), BF16),
            pltpu.VMEM((wide, wide), F32),
        ],
        name="forward",
    )(
        reflectivity.reshape(points // lanes, lanes),
        interleaved_rows(source_green, lanes),
        interleaved_rows(receiver_green, lanes),
    )

    vmem = pl.BlockSpec(memory_space=pltpu.VMEM)
    residual, adj = pl.pallas_call(
        functools.partial(ring_kernel, n, n == 8),
        in_specs=[pl.BlockSpec(memory_space=pltpu.SMEM), vmem, vmem],
        out_specs=[vmem, vmem],
        out_shape=[
            jax.ShapeDtypeStruct(observed.shape, F32),
            jax.ShapeDtypeStruct((freqs, wide, wide), BF16),
        ],
        scratch_shapes=[
            pltpu.VMEM((freqs, 2, 2, per, lanes, lanes), F32),
            pltpu.VMEM((freqs, 2, 2, n // 2, per, lanes, lanes), F32),
            pltpu.VMEM((freqs, 2, n * per, lanes, lanes), BF16),
            pltpu.SemaphoreType.DMA((freqs, 2, 2, n // 2)),
            pltpu.SemaphoreType.DMA((freqs, 2, 2, n // 2)),
            pltpu.SemaphoreType.DMA((freqs, 2, 2, n // 2)),
            pltpu.SemaphoreType.DMA((freqs, 2, 2, n // 2)),
        ],
        compiler_params=pltpu.CompilerParams(collective_id=0, has_side_effects=True),
        name="ring",
    )(table, part, observed)

    gradient = pl.pallas_call(
        adjoint_kernel,
        grid=(tiles, freqs),
        in_specs=[
            pl.BlockSpec((1, TILE, wide), lambda t, f: (f, t, 0)),
            pl.BlockSpec((1, TILE, wide), lambda t, f: (f, t, 0)),
            pl.BlockSpec((freqs, wide, wide), lambda t, f: (0, 0, 0)),
        ],
        out_specs=pl.BlockSpec((TILE // lanes, lanes), lambda t, f: (t, 0)),
        out_shape=jax.ShapeDtypeStruct((points // lanes, lanes), F32),
        scratch_shapes=[pltpu.VMEM((TILE, lanes), F32)],
        name="adjoint",
    )(gd, rd, adj)
    gradient = gradient.reshape(points)
    return (lax.psum_scatter(gradient, "freq", scatter_dimension=0, tiled=True), residual)


def solution(mesh):
    return jax.shard_map(
        on_device,
        mesh=mesh,
        in_specs=(
            P(("parts", "slab")),
            P("freq", ("parts", "slab"), None, None),
            P("freq", ("parts", "slab"), None, None),
            P("freq", ("parts", "slab"), None, None, None),
            P(("parts", "slab"), None),
            P(("parts", "slab"), None),
        ),
        out_specs=(P(("parts", "slab", "freq")), P("freq", ("parts", "slab"), None, None, None)),
        check_vma=False,
    )
```
